32 devices in a mesh: shot: 8 (over z, y), surf: 4 (over x, core).
Axes of the slice: x: 2, y: 2, z: 4, core: 2. Of those that a mesh axis runs over, the one named last changes fastest.
Arguments:
- traces: bfloat16 [64, 1024, 2048], P('shot', 'surf'), may hold values from -6 to 6
- rec_point: int32 [1024], P('surf'), may hold values from 0 to 1023, as said below
- plan: int32 [8], replicated, may hold values from 0 to 7, each once
- green_blocks: bfloat16 [2, 32, 1024, 1024], P(None, 'shot', 'surf'), may hold values from -0.1875 to 0.1875
Outputs:
- multiples: float32 [2, 16, 64, 1024], P(None, None, 'shot', 'surf')
The draws below stay inside these ranges and needn't reach their ends.
Inputs may be any that keep to these rules, and one draw needn't show every extreme that they name: `plan`: each block index appears once; the first 4 entries are used. `rec_point`: receiver r and its surface point p lie in the same one of the equal groups of 256 receivers and 256 surface points, counted in order: p // 256 == r // 256.
All inputs are finite; a program needn't handle non-finite values.
Results may differ from the reference program's by a relative error of at most 0.0029.
Values may be sent and summed in bfloat16 or wider, within the bound.
A program may use at most 128 MiB of HBM per device.

```python
import jax
import jax.numpy as jnp
from jax import lax

S_DEV = 8
R = 1024
X = 1024
T_SIZE = 2048
FB = 4
STEPS = 4
SHOTS = 64
BAND = 32
FREQS = 16
R_DEV = 256
X_DEV = 256
N_SHOT = 8


def draw_rec_point(key, part):
    receiver_groups = jnp.arange(R, dtype=jnp.int32) // R_DEV
    offsets = jax.random.randint(key, (R,), 0, X_DEV, dtype=jnp.int32)
    return (receiver_groups * X_DEV + offsets).astype(jnp.int32)


def shard_levels(rng, extent, pieces, low, top_value):
    gain = 1.0
    for position, blocks in pieces:
        heights = jax.random.uniform(jax.random.fold_in(jax.random.fold_in(rng, 6), position), (blocks,), jnp.float32, low / len(pieces), top_value / len(pieces))
        gain = gain * jnp.repeat(jnp.exp(heights), extent[position] // blocks).reshape((-1,) + (1,) * (len(extent) - 1 - position))
    return gain


def noise(own_key, dims, scale, limit, shards=(), held_as=jnp.bfloat16):
    gain = shard_levels(own_key, dims, shards, -0.22, 0.18) if shards else 1.0
    drawn = jax.random.normal(own_key, dims, jnp.float32) * scale * gain
    return jnp.minimum(jnp.maximum(drawn, -limit), limit).astype(held_as)


def setup_inputs(seed: int = 0) -> dict:
    keys = jax.random.split(jax.random.key(seed), 5)
    traces = noise(keys[0], (SHOTS, R, T_SIZE), 1.0, 6.0, ((0, 8), (1, 4)))
    rec_point = draw_rec_point(jax.random.fold_in(keys[4], 71), 0)
    plan = jax.random.permutation(keys[2], N_SHOT).astype(jnp.int32)
    green_blocks = noise(keys[3], (2, BAND, X, R), X ** -0.5, 0.1875, ((1, 8), (2, 4)))
    return dict(traces=traces, rec_point=rec_point, plan=plan, green_blocks=green_blocks)


def fourier_basis_table(freq_bins):
    times = jnp.arange(T_SIZE, dtype=jnp.int32)
    phases = freq_bins[None, :] * times[:, None] % T_SIZE
    angles = phases.astype(jnp.float32) * (2.0 * jnp.pi / T_SIZE)
    scaling = 1.0 / jnp.sqrt(jnp.float32(T_SIZE))
    return jnp.concatenate([jnp.cos(angles), -jnp.sin(angles)], axis=1) * scaling

def reference(traces, rec_point, plan, green_blocks):
    blocks = plan[:STEPS].astype(jnp.int32)
    frequency_band_rows = (blocks[:, None] * FB + jnp.arange(FB, dtype=jnp.int32)[None, :]).reshape(-1)
    freq_bins = frequency_band_rows + 4
    table = fourier_basis_table(freq_bins)
    grouped = traces.reshape(SHOTS // S_DEV, S_DEV, R, T_SIZE)

    def one_group(shot_rows):
        moved = jnp.transpose(shot_rows, (1, 0, 2)).astype(jnp.float32)
        binned = jax.ops.segment_sum(moved, rec_point, num_segments=X)
        flat = binned.reshape(X * S_DEV, T_SIZE)
        return jnp.dot(flat, table, precision=lax.Precision.HIGHEST).reshape(X, S_DEV, 2 * FREQS)
    spectra = lax.map(one_group, grouped)
    spectra = jnp.transpose(spectra, (1, 0, 2, 3)).reshape(X, SHOTS, 2, FREQS)
    spectra = spectra.astype(jnp.bfloat16).astype(jnp.float32)
    spectra = jnp.transpose(spectra, (2, 3, 1, 0))
    green = green_blocks[:, frequency_band_rows].astype(jnp.float32)
    real_part = jnp.einsum('qsx,qxr->qsr', spectra[0], green[0]) - jnp.einsum('qsx,qxr->qsr', spectra[1], green[1])
    imag_part = jnp.einsum('qsx,qxr->qsr', spectra[0], green[1]) + jnp.einsum('qsx,qxr->qsr', spectra[1], green[0])
    return jnp.stack([real_part, imag_part])
```

```python
import functools

import jax
import jax.numpy as jnp
import numpy as np
from jax import lax
from jax.experimental import pallas as pl
from jax.experimental.pallas import tpu as pltpu
from jax.sharding import PartitionSpec as P

T_SIZE = 2048
FB = 4
STEPS = 4
FIRST_BIN = 4
CHUNKS = 2
HALVES = 2
GROUPS = 2
AHEAD = 4
PAIR = 2
CROSS = 2
SKEW = 5
UNITS = [(g, h, c) for g in range(GROUPS) for h in range(HALVES) for c in range(CHUNKS)]


def basis_table(block_count):
    bins = FIRST_BIN + np.arange(block_count * FB)
    phases = (bins[None, :] * np.arange(T_SIZE)[:, None]) % T_SIZE
    angles = phases * (2.0 * np.pi / T_SIZE)
    table = np.stack([np.cos(angles), -np.sin(angles)], axis=2) / np.sqrt(T_SIZE)
    table = table.reshape(T_SIZE, -1).astype(np.float32)
    high = table.astype(jnp.bfloat16)
    low = (table - high.astype(np.float32)).astype(jnp.bfloat16)
    return np.concatenate([high, low], axis=1)


def kernel(
    n_shot, n_surf,
    plan_hbm, rec_hbm, table_hbm, traces_hbm, green_hbm,
    out_ref,
    plan_ref, rec_ref, table, traces, green, split, outgoing, incoming,
    part, core_in, half_out, half_in, ret_out, ret_in,
    load_sem, trace_sem, green_sem, fwd_send, fwd_recv, core_send, core_recv,
    surf_send, surf_recv, ret_send, ret_recv,
):
    me = lax.axis_index("shot")
    surf = lax.axis_index("surf")
    core = lax.rem(surf, 2)
    row = surf // 2
    n_rows = n_surf // 2
    shots, r_dev, _ = traces.shape
    x_dev = green.shape[2]
    cols = split.shape[1] // 2
    block = 2 * shots
    members = n_shot // GROUPS
    early = n_shot // 4
    part_shots = shots // HALVES
    width = FB // CHUNKS
    run = 2 * part_shots
    mesh_id = pl.DeviceIdType.MESH
    f32, bf16 = jnp.float32, jnp.bfloat16

    order = sorted(range(1, n_shot), key=lambda d: abs(2 * d - n_shot))
    barrier = pltpu.get_barrier_semaphore()
    for d in order:
        pl.semaphore_signal(
            barrier, inc=1, device_id=(lax.rem(me + d, n_shot), surf), device_id_type=mesh_id
        )
    pl.semaphore_signal(
        barrier, inc=1, device_id=(me, row * 2 + 1 - core), device_id_type=mesh_id
    )
    for d in range(1, n_rows):
        pl.semaphore_signal(
            barrier, inc=1, device_id=(me, lax.rem(row + d, n_rows) * 2 + core),
            device_id_type=mesh_id,
        )

    load_rec = pltpu.make_async_copy(rec_hbm, rec_ref, load_sem.at[0])
    load_table = pltpu.make_async_copy(table_hbm, table, load_sem.at[1])
    load_plan = pltpu.make_async_copy(plan_hbm, plan_ref, load_sem.at[2])
    load_rec.start()
    load_table.start()
    loads = [
        pltpu.make_async_copy(traces_hbm.at[s], traces.at[s], trace_sem.at[s])
        for s in range(shots)
    ]
    loads += [
        pltpu.make_async_copy(green_hbm.at[:, j], green.at[:, j], green_sem.at[j])
        for j in range(FB)
    ]
    for s in range(AHEAD):
        loads[s].start()
    load_plan.start()

    load_rec.wait()
    local = rec_ref[...] - surf * x_dev
    hot = (lax.broadcasted_iota(jnp.int32, (x_dev, r_dev), 0) == local).astype(f32).astype(bf16)
    load_table.wait()

    def transform(half):
        for s in range(half * part_shots, (half + 1) * part_shots):
            if s % PAIR == 0:
                for i in range(s, s + PAIR):
                    loads[i].wait()
                    if i + AHEAD < len(loads):
                        loads[i + AHEAD].start()
            both = jnp.dot(traces[s], table[...], preferred_element_type=f32).T
            value = both[:cols] + both[cols:]
            high = value.astype(bf16)
            low = (value - high.astype(f32)).astype(bf16)
            split[s, :cols] = high
            split[s, cols:] = low
        values = split[half * part_shots:(half + 1) * part_shots]
        moved = lax.dot_general(
            values.reshape(part_shots * 2 * cols, r_dev), hot, (((1,), (1,)), ((), ())),
            preferred_element_type=f32,
        ).reshape(part_shots, 2, cols, x_dev)
        spectra = jnp.swapaxes(moved[:, 0] + moved[:, 1], 0, 1)
        outgoing[half] = spectra.reshape(outgoing.shape[1:]).astype(bf16)

    group = me // members

    def send(half):
        for c in range(CHUNKS):
            rows = pl.ds(c * block, block)
            arrived = fwd_recv.at[group, half, c]
            for d in order:
                to = lax.rem(me + d, n_shot)
                pltpu.make_async_remote_copy(
                    outgoing.at[half, to, rows], incoming.at[half, me, rows], fwd_send, arrived,
                    device_id=(to, surf), device_id_type=mesh_id,
                ).start()
            pltpu.make_async_copy(
                outgoing.at[half, me, rows], incoming.at[half, me, rows], arrived
            ).start()

    def enter():
        pl.semaphore_wait(barrier, (n_shot - 1) + 1 + (n_rows - 1))

    transform(0)

    @pl.when(me >= early)
    def _():
        enter()
        send(0)

    transform(1)

    @pl.when(me < early)
    def _():
        enter()
        send(0)

    send(1)

    core_copies, surf_copies = {}, {}
    first_use = [[c for _, _, c in UNITS].index(c) for c in range(CHUNKS)]

    def place(u):
        return UNITS[u]

    def multiply(u):
        g, half, c = place(u)
        span = slice(g * members, (g + 1) * members)
        landed = incoming.at[half, span, c * block:(c + 1) * block]
        pltpu.make_async_copy(landed, landed, fwd_recv.at[g, half, c]).wait()
        spectra = landed[...].astype(f32)
        spectra = spectra.reshape(members, width, 2 * part_shots, x_dev)
        for i in range(width):
            j = c * width + i
            if u == first_use[c]:
                loads[shots + j].wait()
            values = spectra[:, i]
            turned = jnp.concatenate(
                [-values[:, part_shots:], values[:, :part_shots]], axis=1
            )
            values = jnp.concatenate([values, turned], axis=-1)
            values = values.reshape(members * run, 2 * x_dev).astype(bf16)
            for q in range(n_surf):
                operator = green[:, j, :, q * r_dev:(q + 1) * r_dev].reshape(2 * x_dev, r_dev)
                part[u, q % 2, q // 2, i] = jnp.dot(values, operator, preferred_element_type=f32)
        copy = pltpu.make_async_remote_copy(
            part.at[u, 1 - core], core_in.at[u], core_send.at[u], core_recv.at[u],
            device_id=(me, row * 2 + 1 - core), device_id_type=mesh_id,
        )
        copy.start()
        core_copies[u] = copy

    def cross(u):
        core_copies[u].wait_recv()
        surf_copies[u] = []
        for d in range(1, n_rows):
            to = lax.rem(row + d, n_rows)
            half_out[u, d - 1] = (part[u, core, to] + core_in[u, to]).astype(bf16)
            copy = pltpu.make_async_remote_copy(
                half_out.at[u, d - 1], half_in.at[u, d - 1],
                surf_send.at[u, d - 1], surf_recv.at[u, d - 1],
                device_id=(me, to * 2 + core), device_id_type=mesh_id,
            )
            copy.start()
            surf_copies[u].append(copy)

    def give_back(u):
        g, half, c = place(u)
        total = part[u, core, row] + core_in[u, row]
        for d in range(1, n_rows):
            surf_copies[u][d - 1].wait_recv()
            total = total + half_in[u, d - 1].astype(f32)
        total = jnp.swapaxes(total.reshape(width, members, run, r_dev), 0, 1)
        total = total.reshape(members, width * run, r_dev).astype(bf16)
        ret_out[half, c, g * members:(g + 1) * members] = total
        for to in range(g * members, (g + 1) * members):
            @pl.when(to != me)
            def _():
                pltpu.make_async_remote_copy(
                    ret_out.at[half, c, to], ret_in.at[half, c, me], ret_send, ret_recv,
                    device_id=(to, surf), device_id_type=mesh_id,
                ).start()

            @pl.when(to == me)
            def _():
                pltpu.make_async_copy(
                    ret_out.at[half, c, to], ret_in.at[half, c, me], ret_recv
                ).start()

    units = GROUPS * HALVES * CHUNKS
    for t in range(units + SKEW):
        if 0 <= t - CROSS < units:
            cross(t - CROSS)
        if 0 <= t - SKEW < units:
            give_back(t - SKEW)
        if t < units:
            multiply(t)

    load_plan.wait()
    pltpu.make_async_copy(ret_in, ret_in, ret_recv).wait()
    for k in range(STEPS):
        chosen = plan_ref[k]
        for c in range(CHUNKS):
            pieces = [
                ret_in[half, c, chosen].astype(f32).reshape(width, 2, part_shots, r_dev)
                for half in range(HALVES)
            ]
            whole = jnp.concatenate(pieces, axis=2).reshape(width, block, r_dev)
            out_ref[k * FB + c * width:k * FB + (c + 1) * width] = whole.astype(bf16)

    sent = outgoing.at[:, :n_shot - 1]
    pltpu.make_async_copy(sent, sent, fwd_send).wait()
    for u in range(units):
        core_copies[u].wait_send()
        for copy in surf_copies[u]:
            copy.wait_send()
    sent = ret_out.at[:, :, :n_shot - 1]
    pltpu.make_async_copy(sent, sent, ret_send).wait()


def solution(mesh):
    n_shot, n_surf = mesh.shape["shot"], mesh.shape["surf"]
    n_rows = n_surf // 2
    table = basis_table(n_shot)

    def body(traces, rec_point, plan, green):
        shots, r_dev, _ = traces.shape
        x_dev = green.shape[2]
        block = 2 * shots
        cols = n_shot * FB * 2
        units = GROUPS * HALVES * CHUNKS
        unit = (n_rows, FB // CHUNKS, n_shot // GROUPS * block // HALVES, r_dev)
        bf16, f32 = jnp.bfloat16, jnp.float32
        dma = pltpu.SemaphoreType.DMA
        whole = pl.BlockSpec(memory_space=pltpu.HBM)
        chosen = pl.pallas_call(
            functools.partial(kernel, n_shot, n_surf),
            out_shape=jax.ShapeDtypeStruct((STEPS * FB, block, r_dev), bf16),
            in_specs=[whole] * 5,
            out_specs=pl.BlockSpec(memory_space=pltpu.VMEM),
            scratch_shapes=[
                pltpu.SMEM(plan.shape, jnp.int32),
                pltpu.VMEM((1, r_dev), jnp.int32),
                pltpu.VMEM(table.shape, bf16),
                pltpu.VMEM(traces.shape, bf16),
                pltpu.VMEM(green.shape, bf16),
                pltpu.VMEM((shots, 2 * cols, r_dev), bf16),
                pltpu.VMEM((HALVES, n_shot, CHUNKS * block, x_dev), bf16),
                pltpu.VMEM((HALVES, n_shot, CHUNKS * block, x_dev), bf16),
                pltpu.VMEM((units, 2) + unit, f32),
                pltpu.VMEM((units,) + unit, f32),
                pltpu.VMEM((units, n_rows - 1) + unit[1:], bf16),
                pltpu.VMEM((units, n_rows - 1) + unit[1:], bf16),
                pltpu.VMEM((HALVES, CHUNKS, n_shot, block, r_dev), bf16),
                pltpu.VMEM((HALVES, CHUNKS, n_shot, block, r_dev), bf16),
                dma((3,)),
                dma((shots,)),
                dma((FB,)),
                dma, dma((GROUPS, HALVES, CHUNKS)),
                dma((units,)), dma((units,)),
                dma((units, n_rows)), dma((units, n_rows)),
                dma, dma,
            ],
            compiler_params=pltpu.CompilerParams(
                collective_id=0, has_side_effects=True, vmem_limit_bytes=48 << 20
            ),
        )(*[pltpu.with_memory_space_constraint(v, pltpu.HBM) for v in (plan, rec_point.reshape(1, r_dev), jnp.asarray(table), traces, green)])
        chosen = chosen.reshape(STEPS * FB, 2, shots, r_dev).astype(f32)
        return jnp.swapaxes(chosen, 0, 1)

    in_specs = (P("shot", "surf", None), P("surf"), P(), P(None, "shot", "surf", None))
    out_specs = P(None, None, "shot", "surf")
    return jax.shard_map(body, mesh=mesh, in_specs=in_specs, out_specs=out_specs, check_vma=False)
```

```python
import functools

import jax
import jax.numpy as jnp
import numpy as np
from jax import lax
from jax.experimental import pallas as pl
from jax.experimental.pallas import tpu as pltpu
from jax.sharding import PartitionSpec as P

T_SIZE = 2048
FB = 4
STEPS = 4
FIRST_BIN = 4
CHUNKS = 2
HALVES = 2
GROUPS = 2
AHEAD = 4
PAIR = 2
CROSS = 2
SKEW = 5


def basis_table(block_count):
    bins = FIRST_BIN + np.arange(block_count * FB)
    phases = (bins[None, :] * np.arange(T_SIZE)[:, None]) % T_SIZE
    angles = phases * (2.0 * np.pi / T_SIZE)
    table = np.stack([np.cos(angles), -np.sin(angles)], axis=2) / np.sqrt(T_SIZE)
    table = table.reshape(T_SIZE, -1).astype(np.float32)
    high = table.astype(jnp.bfloat16)
    low = (table - high.astype(np.float32)).astype(jnp.bfloat16)
    return np.concatenate([high, low], axis=1)


def kernel(
    n_shot, n_surf,
    plan_hbm, rec_hbm, table_hbm, traces_hbm, green_hbm,
    out_ref,
    plan_ref, rec_ref, table, traces, green, split, outgoing, incoming,
    part, core_in, half_out, half_in, ret_out, ret_in,
    load_sem, trace_sem, green_sem, fwd_send, fwd_recv, core_send, core_recv,
    surf_send, surf_recv, ret_send, ret_recv,
):
    me = lax.axis_index("shot")
    surf = lax.axis_index("surf")
    core = lax.rem(surf, 2)
    row = surf // 2
    n_rows = n_surf // 2
    shots, r_dev, _ = traces.shape
    x_dev = green.shape[2]
    cols = split.shape[1] // 2
    block = 2 * shots
    members = n_shot // GROUPS
    early = n_shot // 4
    part_shots = shots // HALVES
    width = FB // CHUNKS
    run = 2 * part_shots
    mesh_id = pl.DeviceIdType.MESH
    f32, bf16 = jnp.float32, jnp.bfloat16

    order = sorted(range(1, n_shot), key=lambda d: abs(2 * d - n_shot))
    barrier = pltpu.get_barrier_semaphore()
    for d in order:
        pl.semaphore_signal(
            barrier, inc=1, device_id=(lax.rem(me + d, n_shot), surf), device_id_type=mesh_id
        )
    pl.semaphore_signal(
        barrier, inc=1, device_id=(me, row * 2 + 1 - core), device_id_type=mesh_id
    )
    for d in range(1, n_rows):
        pl.semaphore_signal(
            barrier, inc=1, device_id=(me, lax.rem(row + d, n_rows) * 2 + core),
            device_id_type=mesh_id,
        )

    load_rec = pltpu.make_async_copy(rec_hbm, rec_ref, load_sem.at[0])
    load_table = pltpu.make_async_copy(table_hbm, table, load_sem.at[1])
    load_plan = pltpu.make_async_copy(plan_hbm, plan_ref, load_sem.at[2])
    load_rec.start()
    load_table.start()
    loads = [
        pltpu.make_async_copy(traces_hbm.at[s], traces.at[s], trace_sem.at[s])
        for s in range(shots)
    ]
    loads += [
        pltpu.make_async_copy(green_hbm.at[:, j], green.at[:, j], green_sem.at[j])
        for j in range(FB)
    ]
    for s in range(AHEAD):
        loads[s].start()
    load_plan.start()

    load_rec.wait()
    local = rec_ref[...] - surf * x_dev
    hot = (lax.broadcasted_iota(jnp.int32, (x_dev, r_dev), 0) == local).astype(f32).astype(bf16)
    load_table.wait()

    def transform(half):
        for s in range(half * part_shots, (half + 1) * part_shots):
            if s % PAIR == 0:
                for i in range(s, s + PAIR):
                    loads[i].wait()
                    if i + AHEAD < len(loads):
                        loads[i + AHEAD].start()
            both = jnp.dot(traces[s], table[...], preferred_element_type=f32).T
            value = both[:cols] + both[cols:]
            high = value.astype(bf16)
            low = (value - high.astype(f32)).astype(bf16)
            split[s, :cols] = high
            split[s, cols:] = low
        values = split[half * part_shots:(half + 1) * part_shots]
        moved = lax.dot_general(
            values.reshape(part_shots * 2 * cols, r_dev), hot, (((1,), (1,)), ((), ())),
            preferred_element_type=f32,
        ).reshape(part_shots, 2, cols, x_dev)
        spectra = jnp.swapaxes(moved[:, 0] + moved[:, 1], 0, 1)
        outgoing[half] = spectra.reshape(outgoing.shape[1:]).astype(bf16)

    group = me // members

    def send(half):
        for c in range(CHUNKS):
            rows = pl.ds(c * block, block)
            arrived = fwd_recv.at[group, half, c]
            for d in order:
                to = lax.rem(me + d, n_shot)
                pltpu.make_async_remote_copy(
                    outgoing.at[half, to, rows], incoming.at[half, me, rows], fwd_send, arrived,
                    device_id=(to, surf), device_id_type=mesh_id,
                ).start()
            pltpu.make_async_copy(
                outgoing.at[half, me, rows], incoming.at[half, me, rows], arrived
            ).start()

    def enter():
        pl.semaphore_wait(barrier, (n_shot - 1) + 1 + (n_rows - 1))

    transform(0)

    @pl.when(me >= early)
    def _():
        enter()
        send(0)

    transform(1)

    @pl.when(me < early)
    def _():
        enter()
        send(0)

    send(1)

    core_copies, surf_copies = {}, {}
    far = me // (n_shot // 2)

    def place(u):
        turn, c = u // CHUNKS, u % CHUNKS
        by_group, by_half = divmod(turn, HALVES), divmod(turn, GROUPS)[::-1]
        g, half = (far * a + (1 - far) * b for a, b in zip(by_group, by_half))
        return g, half, c

    def multiply(u):
        g, half, c = place(u)
        span = pl.ds(g * members, members)
        landed = incoming.at[half, span, c * block:(c + 1) * block]
        pltpu.make_async_copy(landed, landed, fwd_recv.at[g, half, c]).wait()
        spectra = landed[...].astype(f32)
        spectra = spectra.reshape(members, width, 2 * part_shots, x_dev)
        for i in range(width):
            j = c * width + i
            if u < CHUNKS:
                loads[shots + j].wait()
            values = spectra[:, i]
            turned = jnp.concatenate(
                [-values[:, part_shots:], values[:, :part_shots]], axis=1
            )
            values = jnp.concatenate([values, turned], axis=-1)
            values = values.reshape(members * run, 2 * x_dev).astype(bf16)
            for q in range(n_surf):
                operator = green[:, j, :, q * r_dev:(q + 1) * r_dev].reshape(2 * x_dev, r_dev)
                part[u, q % 2, q // 2, i] = jnp.dot(values, operator, preferred_element_type=f32)
        copy = pltpu.make_async_remote_copy(
            part.at[u, 1 - core], core_in.at[u], core_send.at[u], core_recv.at[u],
            device_id=(me, row * 2 + 1 - core), device_id_type=mesh_id,
        )
        copy.start()
        core_copies[u] = copy

    def cross(u):
        core_copies[u].wait_recv()
        surf_copies[u] = []
        for d in range(1, n_rows):
            to = lax.rem(row + d, n_rows)
            half_out[u, d - 1] = (part[u, core, to] + core_in[u, to]).astype(bf16)
            copy = pltpu.make_async_remote_copy(
                half_out.at[u, d - 1], half_in.at[u, d - 1],
                surf_send.at[u, d - 1], surf_recv.at[u, d - 1],
                device_id=(me, to * 2 + core), device_id_type=mesh_id,
            )
            copy.start()
            surf_copies[u].append(copy)

    def give_back(u):
        g, half, c = place(u)
        total = part[u, core, row] + core_in[u, row]
        for d in range(1, n_rows):
            surf_copies[u][d - 1].wait_recv()
            total = total + half_in[u, d - 1].astype(f32)
        total = jnp.swapaxes(total.reshape(width, members, run, r_dev), 0, 1)
        total = total.reshape(members, width * run, r_dev).astype(bf16)
        ret_out[half, c, pl.ds(g * members, members)] = total
        for i in range(members):
            to = g * members + i

            @pl.when(to != me)
            def _():
                pltpu.make_async_remote_copy(
                    ret_out.at[half, c, to], ret_in.at[half, c, me], ret_send, ret_recv,
                    device_id=(to, surf), device_id_type=mesh_id,
                ).start()

            @pl.when(to == me)
            def _():
                pltpu.make_async_copy(
                    ret_out.at[half, c, to], ret_in.at[half, c, me], ret_recv
                ).start()

    units = GROUPS * HALVES * CHUNKS
    for t in range(units + SKEW):
        if 0 <= t - CROSS < units:
            cross(t - CROSS)
        if 0 <= t - SKEW < units:
            give_back(t - SKEW)
        if t < units:
            multiply(t)

    load_plan.wait()
    pltpu.make_async_copy(ret_in, ret_in, ret_recv).wait()
    for k in range(STEPS):
        chosen = plan_ref[k]
        for c in range(CHUNKS):
            pieces = [
                ret_in[half, c, chosen].astype(f32).reshape(width, 2, part_shots, r_dev)
                for half in range(HALVES)
            ]
            whole = jnp.concatenate(pieces, axis=2).reshape(width, block, r_dev)
            out_ref[k * FB + c * width:k * FB + (c + 1) * width] = whole.astype(bf16)

    sent = outgoing.at[:, :n_shot - 1]
    pltpu.make_async_copy(sent, sent, fwd_send).wait()
    for u in range(units):
        core_copies[u].wait_send()
        for copy in surf_copies[u]:
            copy.wait_send()
    sent = ret_out.at[:, :, :n_shot - 1]
    pltpu.make_async_copy(sent, sent, ret_send).wait()


def solution(mesh):
    n_shot, n_surf = mesh.shape["shot"], mesh.shape["surf"]
    n_rows = n_surf // 2
    table = basis_table(n_shot)

    def body(traces, rec_point, plan, green):
        shots, r_dev, _ = traces.shape
        x_dev = green.shape[2]
        block = 2 * shots
        cols = n_shot * FB * 2
        units = GROUPS * HALVES * CHUNKS
        unit = (n_rows, FB // CHUNKS, n_shot // GROUPS * block // HALVES, r_dev)
        bf16, f32 = jnp.bfloat16, jnp.float32
        dma = pltpu.SemaphoreType.DMA
        whole = pl.BlockSpec(memory_space=pltpu.HBM)
        chosen = pl.pallas_call(
            functools.partial(kernel, n_shot, n_surf),
            out_shape=jax.ShapeDtypeStruct((STEPS * FB, block, r_dev), bf16),
            in_specs=[whole] * 5,
            out_specs=pl.BlockSpec(memory_space=pltpu.VMEM),
            scratch_shapes=[
                pltpu.SMEM(plan.shape, jnp.int32),
                pltpu.VMEM((1, r_dev), jnp.int32),
                pltpu.VMEM(table.shape, bf16),
                pltpu.VMEM(traces.shape, bf16),
                pltpu.VMEM(green.shape, bf16),
                pltpu.VMEM((shots, 2 * cols, r_dev), bf16),
                pltpu.VMEM((HALVES, n_shot, CHUNKS * block, x_dev), bf16),
                pltpu.VMEM((HALVES, n_shot, CHUNKS * block, x_dev), bf16),
                pltpu.VMEM((units, 2) + unit, f32),
                pltpu.VMEM((units,) + unit, f32),
                pltpu.VMEM((units, n_rows - 1) + unit[1:], bf16),
                pltpu.VMEM((units, n_rows - 1) + unit[1:], bf16),
                pltpu.VMEM((HALVES, CHUNKS, n_shot, block, r_dev), bf16),
                pltpu.VMEM((HALVES, CHUNKS, n_shot, block, r_dev), bf16),
                dma((3,)),
                dma((shots,)),
                dma((FB,)),
                dma, dma((GROUPS, HALVES, CHUNKS)),
                dma((units,)), dma((units,)),
                dma((units, n_rows)), dma((units, n_rows)),
                dma, dma,
            ],
            compiler_params=pltpu.CompilerParams(
                collective_id=0, has_side_effects=True, vmem_limit_bytes=48 << 20
            ),
        )(*[pltpu.with_memory_space_constraint(v, pltpu.HBM) for v in (plan, rec_point.reshape(1, r_dev), jnp.asarray(table), traces, green)])
        chosen = chosen.reshape(STEPS * FB, 2, shots, r_dev).astype(f32)
        return jnp.swapaxes(chosen, 0, 1)

    in_specs = (P("shot", "surf", None), P("surf"), P(), P(None, "shot", "surf", None))
    out_specs = P(None, None, "shot", "surf")
    return jax.shard_map(body, mesh=mesh, in_specs=in_specs, out_specs=out_specs, check_vma=False)
```

```python
import functools

import jax
import jax.numpy as jnp
import numpy as np
from jax import lax
from jax.experimental import pallas as pl
from jax.experimental.pallas import tpu as pltpu
from jax.sharding import PartitionSpec as P

T_SIZE = 2048
FB = 4
STEPS = 4
FIRST_BIN = 4
CHUNKS = 2
HALVES = 2
GROUPS = 2
AHEAD = 4
PAIR = 2
CROSS = 2
SKEW = 5


def basis_table(block_count):
    bins = FIRST_BIN + np.arange(block_count * FB)
    phases = (bins[None, :] * np.arange(T_SIZE)[:, None]) % T_SIZE
    angles = phases * (2.0 * np.pi / T_SIZE)
    table = np.stack([np.cos(angles), -np.sin(angles)], axis=2) / np.sqrt(T_SIZE)
    table = table.reshape(T_SIZE, -1).astype(np.float32)
    high = table.astype(jnp.bfloat16)
    low = (table - high.astype(np.float32)).astype(jnp.bfloat16)
    return np.concatenate([high, low], axis=1)


def kernel(
    n_shot, n_surf,
    plan_hbm, rec_hbm, table_hbm, traces_hbm, green_hbm,
    out_ref,
    plan_ref, rec_ref, table, traces, green, split, outgoing, incoming,
    part, core_in, half_out, half_in, ret_out, ret_in_a, ret_in_b,
    load_sem, trace_sem, green_sem, fwd_send, fwd_recv, core_send, core_recv,
    surf_send, surf_recv, ret_send, ret_recv,
):
    me = lax.axis_index("shot")
    surf = lax.axis_index("surf")
    core = lax.rem(surf, 2)
    row = surf // 2
    n_rows = n_surf // 2
    shots, r_dev, _ = traces.shape
    x_dev = green.shape[2]
    cols = split.shape[1] // 2
    block = 2 * shots
    members = n_shot // GROUPS
    ret_in = (ret_in_a, ret_in_b)
    early = n_shot // 4
    part_shots = shots // HALVES
    width = FB // CHUNKS
    run = 2 * part_shots
    mesh_id = pl.DeviceIdType.MESH
    f32, bf16 = jnp.float32, jnp.bfloat16

    order = sorted(range(1, n_shot), key=lambda d: abs(2 * d - n_shot))
    barrier = pltpu.get_barrier_semaphore()
    for d in order:
        pl.semaphore_signal(
            barrier, inc=1, device_id=(lax.rem(me + d, n_shot), surf), device_id_type=mesh_id
        )
    pl.semaphore_signal(
        barrier, inc=1, device_id=(me, row * 2 + 1 - core), device_id_type=mesh_id
    )
    for d in range(1, n_rows):
        pl.semaphore_signal(
            barrier, inc=1, device_id=(me, lax.rem(row + d, n_rows) * 2 + core),
            device_id_type=mesh_id,
        )

    load_rec = pltpu.make_async_copy(rec_hbm, rec_ref, load_sem.at[0])
    load_table = pltpu.make_async_copy(table_hbm, table, load_sem.at[1])
    load_plan = pltpu.make_async_copy(plan_hbm, plan_ref, load_sem.at[2])
    load_rec.start()
    load_table.start()
    loads = [
        pltpu.make_async_copy(traces_hbm.at[s], traces.at[s], trace_sem.at[s])
        for s in range(shots)
    ]
    loads += [
        pltpu.make_async_copy(green_hbm.at[:, j], green.at[:, j], green_sem.at[j])
        for j in range(FB)
    ]
    for s in range(AHEAD):
        loads[s].start()
    load_plan.start()

    load_rec.wait()
    local = rec_ref[...] - surf * x_dev
    hot = (lax.broadcasted_iota(jnp.int32, (x_dev, r_dev), 0) == local).astype(f32).astype(bf16)
    load_table.wait()

    def transform(half):
        for s in range(half * part_shots, (half + 1) * part_shots):
            if s % PAIR == 0:
                for i in range(s, s + PAIR):
                    loads[i].wait()
                    if i + AHEAD < len(loads):
                        loads[i + AHEAD].start()
            both = jnp.dot(traces[s], table[...], preferred_element_type=f32).T
            value = both[:cols] + both[cols:]
            high = value.astype(bf16)
            low = (value - high.astype(f32)).astype(bf16)
            split[s, :cols] = high
            split[s, cols:] = low
        values = split[half * part_shots:(half + 1) * part_shots]
        moved = lax.dot_general(
            values.reshape(part_shots * 2 * cols, r_dev), hot, (((1,), (1,)), ((), ())),
            preferred_element_type=f32,
        ).reshape(part_shots, 2, cols, x_dev)
        spectra = jnp.swapaxes(moved[:, 0] + moved[:, 1], 0, 1)
        outgoing[half] = spectra.reshape(outgoing.shape[1:]).astype(bf16)

    group = me // members

    def send(half):
        for c in range(CHUNKS):
            rows = pl.ds(c * block, block)
            arrived = fwd_recv.at[group, half, c]
            for d in order:
                to = lax.rem(me + d, n_shot)
                pltpu.make_async_remote_copy(
                    outgoing.at[half, to, rows], incoming.at[half, me, rows], fwd_send, arrived,
                    device_id=(to, surf), device_id_type=mesh_id,
                ).start()
            pltpu.make_async_copy(
                outgoing.at[half, me, rows], incoming.at[half, me, rows], arrived
            ).start()

    def enter():
        pl.semaphore_wait(barrier, (n_shot - 1) + 1 + (n_rows - 1))

    transform(0)

    @pl.when(me >= early)
    def _():
        enter()
        send(0)

    transform(1)

    @pl.when(me < early)
    def _():
        enter()
        send(0)

    send(1)

    core_copies, surf_copies = {}, {}
    far = me // (n_shot // 2)

    def place(u):
        turn, c = u // CHUNKS, u % CHUNKS
        by_group, by_half = divmod(turn, HALVES), divmod(turn, GROUPS)[::-1]
        g, half = (far * a + (1 - far) * b for a, b in zip(by_group, by_half))
        return g, half, c

    def multiply(u):
        g, half, c = place(u)
        span = pl.ds(g * members, members)
        landed = incoming.at[half, span, c * block:(c + 1) * block]
        pltpu.make_async_copy(landed, landed, fwd_recv.at[g, half, c]).wait()
        spectra = landed[...].astype(f32)
        spectra = spectra.reshape(members, width, 2 * part_shots, x_dev)
        for i in range(width):
            j = c * width + i
            if u < CHUNKS:
                loads[shots + j].wait()
            values = spectra[:, i]
            turned = jnp.concatenate(
                [-values[:, part_shots:], values[:, :part_shots]], axis=1
            )
            values = jnp.concatenate([values, turned], axis=-1)
            values = values.reshape(members * run, 2 * x_dev).astype(bf16)
            for q in range(n_surf):
                operator = green[:, j, :, q * r_dev:(q + 1) * r_dev].reshape(2 * x_dev, r_dev)
                part[u, q % 2, q // 2, i] = jnp.dot(values, operator, preferred_element_type=f32)
        copy = pltpu.make_async_remote_copy(
            part.at[u, 1 - core], core_in.at[u], core_send.at[u], core_recv.at[u],
            device_id=(me, row * 2 + 1 - core), device_id_type=mesh_id,
        )
        copy.start()
        core_copies[u] = copy

    def cross(u):
        core_copies[u].wait_recv()
        surf_copies[u] = []
        for d in range(1, n_rows):
            to = lax.rem(row + d, n_rows)
            half_out[u, d - 1] = (part[u, core, to] + core_in[u, to]).astype(bf16)
            copy = pltpu.make_async_remote_copy(
                half_out.at[u, d - 1], half_in.at[u, d - 1],
                surf_send.at[u, d - 1], surf_recv.at[u, d - 1],
                device_id=(me, to * 2 + core), device_id_type=mesh_id,
            )
            copy.start()
            surf_copies[u].append(copy)

    def give_back(u):
        g, half, c = place(u)
        total = part[u, core, row] + core_in[u, row]
        for d in range(1, n_rows):
            surf_copies[u][d - 1].wait_recv()
            total = total + half_in[u, d - 1].astype(f32)
        total = jnp.swapaxes(total.reshape(width, members, run, r_dev), 0, 1)
        total = total.reshape(members, width * run, r_dev).astype(bf16)
        ret_out[half, c, pl.ds(g * members, members)] = total
        for i in range(members):
            to = g * members + i

            @pl.when(to != me)
            def _():
                pltpu.make_async_remote_copy(
                    ret_out.at[half, c, to], ret_in[c].at[half, me], ret_send, ret_recv.at[c],
                    device_id=(to, surf), device_id_type=mesh_id,
                ).start()

            @pl.when(to == me)
            def _():
                pltpu.make_async_copy(
                    ret_out.at[half, c, to], ret_in[c].at[half, me], ret_recv.at[c]
                ).start()

    units = GROUPS * HALVES * CHUNKS
    for t in range(units + SKEW):
        if 0 <= t - CROSS < units:
            cross(t - CROSS)
        if 0 <= t - SKEW < units:
            give_back(t - SKEW)
        if t < units:
            multiply(t)

    load_plan.wait()
    for c in range(CHUNKS):
        returned = ret_in[c]
        pltpu.make_async_copy(returned, returned, ret_recv.at[c]).wait()
        for k in range(STEPS):
            chosen = plan_ref[k]
            pieces = [
                ret_in[c][half, chosen].astype(f32).reshape(width, 2, part_shots, r_dev)
                for half in range(HALVES)
            ]
            whole = jnp.concatenate(pieces, axis=2)
            for i in range(width):
                out_ref[:, k * FB + c * width + i] = whole[i]

    sent = outgoing.at[:, :n_shot - 1]
    pltpu.make_async_copy(sent, sent, fwd_send).wait()
    for u in range(units):
        core_copies[u].wait_send()
        for copy in surf_copies[u]:
            copy.wait_send()
    sent = ret_out.at[:, :, :n_shot - 1]
    pltpu.make_async_copy(sent, sent, ret_send).wait()


def solution(mesh):
    n_shot, n_surf = mesh.shape["shot"], mesh.shape["surf"]
    n_rows = n_surf // 2
    table = basis_table(n_shot)

    def body(traces, rec_point, plan, green):
        shots, r_dev, _ = traces.shape
        x_dev = green.shape[2]
        block = 2 * shots
        cols = n_shot * FB * 2
        units = GROUPS * HALVES * CHUNKS
        unit = (n_rows, FB // CHUNKS, n_shot // GROUPS * block // HALVES, r_dev)
        bf16, f32 = jnp.bfloat16, jnp.float32
        dma = pltpu.SemaphoreType.DMA
        whole = pl.BlockSpec(memory_space=pltpu.HBM)
        chosen = pl.pallas_call(
            functools.partial(kernel, n_shot, n_surf),
            out_shape=jax.ShapeDtypeStruct((2, STEPS * FB, shots, r_dev), f32),
            in_specs=[whole] * 5,
            out_specs=pl.BlockSpec(memory_space=pltpu.VMEM),
            scratch_shapes=[
                pltpu.SMEM(plan.shape, jnp.int32),
                pltpu.VMEM((1, r_dev), jnp.int32),
                pltpu.VMEM(table.shape, bf16),
                pltpu.VMEM(traces.shape, bf16),
                pltpu.VMEM(green.shape, bf16),
                pltpu.VMEM((shots, 2 * cols, r_dev), bf16),
                pltpu.VMEM((HALVES, n_shot, CHUNKS * block, x_dev), bf16),
                pltpu.VMEM((HALVES, n_shot, CHUNKS * block, x_dev), bf16),
                pltpu.VMEM((units, 2) + unit, f32),
                pltpu.VMEM((units,) + unit, f32),
                pltpu.VMEM((units, n_rows - 1) + unit[1:], bf16),
                pltpu.VMEM((units, n_rows - 1) + unit[1:], bf16),
                pltpu.VMEM((HALVES, CHUNKS, n_shot, block, r_dev), bf16),
                pltpu.VMEM((HALVES, n_shot, block, r_dev), bf16),
                pltpu.VMEM((HALVES, n_shot, block, r_dev), bf16),
                dma((3,)),
                dma((shots,)),
                dma((FB,)),
                dma, dma((GROUPS, HALVES, CHUNKS)),
                dma((units,)), dma((units,)),
                dma((units, n_rows)), dma((units, n_rows)),
                dma, dma((CHUNKS,)),
            ],
            compiler_params=pltpu.CompilerParams(
                collective_id=0, has_side_effects=True, vmem_limit_bytes=48 << 20
            ),
        )(*[pltpu.with_memory_space_constraint(v, pltpu.HBM) for v in (plan, rec_point.reshape(1, r_dev), jnp.asarray(table), traces, green)])
        return chosen

    in_specs = (P("shot", "surf", None), P("surf"), P(), P(None, "shot", "surf", None))
    out_specs = P(None, None, "shot", "surf")
    return jax.shard_map(body, mesh=mesh, in_specs=in_specs, out_specs=out_specs, check_vma=False)
```
